256 devices in a mesh: node: 32 (over x_hi, z, core), tone: 8 (over x_lo, y).
Axes of the slice: x: 4 (x_hi: 2, x_lo: 2; x = x_hi * 2 + x_lo), y: 4, z: 8, core: 2. Of those that a mesh axis runs over, the one named last changes fastest.
Arguments:
- voltages: float32 [32, 32, 32768], P(None, 'tone', 'node'), may hold values from -6 to 6
- source: float32 [32, 32, 32768], P(None, 'tone', 'node'), may hold values from -6 to 6
- coupling: float32 [256, 7, 128, 128], P('node'), may hold values from -0.1875 to 0.1875
- band_code: int32 [7], replicated, may hold values from 0 to 6, each once
- active: int32 [256, 7], P('node'), may hold values 0 or 1
- cap: float32 [32768], P('node'), may hold values from 0.5 to 2
- damp: float32 [32, 32], P(None, 'tone'), may hold values from 0.5 to 4
- kind: int32 [32768], P('node'), may hold values from 0 to 3
- type_params: float32 [3, 4], replicated, may hold values from 0.3 to 2
Outputs:
- new_voltages: float32 [32, 32, 32768], P(None, 'tone', 'node')
- remaining: float32 [32, 32, 32768], P(None, 'tone', 'node')
The draws below stay inside these ranges and needn't reach their ends.
Inputs may be any that keep to these rules, and one draw needn't show every extreme that they name: band_code holds each of 0 to 6 once, so the bands reach every block offset from -3 to 3.
All inputs are finite; a program needn't handle non-finite values. No bound on the sum of `active` on one device may be relied on, other than what follows from the above.
Results may differ from the reference program's by a relative error of at most 0.0003.
Values sent between devices are 32-bit elements; how exact they have to be, the bound alone decides.
A program may use at most 128 MiB of HBM per device.

```python
import math
import jax
import jax.numpy as jnp
from jax import lax

K1 = 32
K2 = 32
NB = 128
HALO_B = 3
NOFF = 7
M = 4
NTYPES = 4
NODES = 32768
NBLOCKS = 256


def set_ends(entries, key, low, largest):
    place = [jax.random.randint(jax.random.fold_in(key, axis), (), 0, length) for axis, length in enumerate(entries.shape)]
    longest = entries.shape.index(max(entries.shape))
    beside = place[:longest] + [(place[longest] + 1) % entries.shape[longest]] + place[longest + 1:]
    return entries.at[tuple(place)].set(low).at[tuple(beside)].set(largest)


def level_of(rng, dims, pieces, low, high):
    loudness = 1.0
    for position, blocks in pieces:
        steps = jax.random.uniform(jax.random.fold_in(jax.random.fold_in(rng, 6), position), (blocks,), jnp.float32, low / len(pieces), high / len(pieces))
        loudness = loudness * jnp.repeat(jnp.exp(steps), dims[position] // blocks).reshape((-1,) + (1,) * (len(dims) - 1 - position))
    return loudness


def scatter_about(own_key, dims, width, limit, shards=(), kind=jnp.bfloat16):
    array = width * jax.random.normal(own_key, dims, jnp.float32)
    if shards:
        array = array * level_of(own_key, dims, shards, -0.22, 0.18)
    return jnp.clip(array, -limit, limit).astype(kind)


def setup_inputs(seed: int = 0) -> dict:
    keys = jax.random.split(jax.random.key(seed), 10)
    voltages = scatter_about(keys[0], (K1, K2, NODES), 1.0, 6.0, ((1, 8), (2, 32)), jnp.float32)
    source = scatter_about(keys[1], (K1, K2, NODES), 1.0, 6.0, ((1, 8), (2, 32)), jnp.float32)
    coupling = scatter_about(keys[2], (NBLOCKS, NOFF, NB, NB), (NB * NOFF) ** -0.5, 0.1875, ((0, 32),), jnp.float32)
    band_code = jax.random.permutation(keys[3], NOFF).astype(jnp.int32)
    active = set_ends((jax.random.randint(keys[4], (NBLOCKS, NOFF), 0, 4) < 3).astype(jnp.int32), jax.random.fold_in(keys[4], 1), 0, 1)
    cap = jnp.clip(jnp.exp(math.log(2.0) - 1.3862944 * jax.random.uniform(keys[5], (NODES,), jnp.float32) ** level_of(keys[5], (NODES,), ((0, 32),), -0.2, 0.2)), 0.5, 2.0)
    damp = jnp.clip(jnp.exp(math.log(4.0) - 2.0794415 * jax.random.uniform(keys[6], (K1, K2), jnp.float32) ** level_of(keys[6], (K1, K2), ((1, 8),), -0.2, 0.2)), 0.5, 4.0)
    kind = set_ends(jax.random.randint(keys[7], (NODES,), 0, NTYPES), jax.random.fold_in(keys[7], 1), 0, NTYPES - 1).astype(jnp.int32)
    type_params = jnp.clip(jnp.exp(jax.random.uniform(keys[8], (3, NTYPES), jnp.float32, math.log(0.3), math.log(2.0))), 0.3, 2.0)
    return dict(voltages=voltages, source=source, coupling=coupling, band_code=band_code, active=active, cap=cap, damp=damp, kind=kind, type_params=type_params)


HIGH = lax.Precision.HIGHEST

def hartley(count):
    grid = jnp.arange(count, dtype=jnp.int32)
    phase = grid[:, None] * grid[None, :] % count
    angle = phase.astype(jnp.float32) * (2.0 * math.pi / count)
    return (jnp.cos(angle) + jnp.sin(angle)) / math.sqrt(count)

def transform(field, first, second):
    field = jnp.einsum('tk,kqn->tqn', first, field, precision=HIGH)
    return jnp.einsum('sq,tqn->tsn', second, field, precision=HIGH)

def couple(field, masked, band_code, scale):
    nodes = field.shape[2]
    blocks = nodes // NB
    reach = HALO_B * NB
    padded = jnp.pad(field, ((0, 0), (0, 0), (reach, reach)))
    rows = field.shape[0] * field.shape[1]
    total = scale * field
    for band in range(NOFF):
        begin = (band_code[band] * NB).astype(jnp.int32)
        source = lax.dynamic_slice_in_dim(padded, begin, nodes, 2)
        term = jnp.einsum('rbc,bsc->rbs', source.reshape(rows, blocks, NB), masked[:, band], precision=HIGH)
        total = total + term.reshape(field.shape)
    return total

def small_solve(gram, rhs):
    lower = jnp.linalg.cholesky(gram)
    count = rhs.shape[0]
    forward = []
    for index in range(count):
        total = rhs[index]
        for other in range(index):
            total = total - lower[index, other] * forward[other]
        forward.append(total / lower[index, index])
    backward = [None] * count
    for index in reversed(range(count)):
        total = forward[index]
        for other in range(index + 1, count):
            total = total - lower[other, index] * backward[other]
        backward[index] = total / lower[index, index]
    return jnp.stack(backward)

def reference(voltages, source, coupling, band_code, active, cap, damp, kind, type_params):
    first = hartley(K1)
    second = hartley(K2)
    onehot = (kind[None, :] == jnp.arange(NTYPES, dtype=jnp.int32)[:, None]).astype(type_params.dtype)
    per_node = jnp.dot(type_params, onehot, precision=HIGH)
    linear, amplitude, sharpness = (per_node[0], per_node[1], per_node[2])
    masked = coupling * active[:, :, None, None].astype(coupling.dtype)
    scale = damp[:, :, None] * cap[None, None, :]
    wave = transform(voltages, first, second)
    bend = jnp.tanh(sharpness * wave)
    current = linear * wave + amplitude * bend
    slope = linear + amplitude * sharpness * (1.0 - bend * bend)
    start = source - couple(voltages, masked, band_code, scale) - transform(current, first, second)

    def jacobian(field):
        return couple(field, masked, band_code, scale) + transform(slope * transform(field, first, second), first, second)
    beta = jnp.sqrt(jnp.sum(start * start))
    basis = [start / beta]
    hessen = jnp.zeros((M + 1, M), dtype=start.dtype)
    for column in range(M):
        image = jacobian(basis[column])
        projected = jnp.stack([jnp.sum(vector * image) for vector in basis])
        for index in range(len(basis)):
            image = image - projected[index] * basis[index]
        length = jnp.sqrt(jnp.sum(image * image))
        hessen = hessen.at[:column + 1, column].set(projected)
        hessen = hessen.at[column + 1, column].set(length)
        basis.append(image / length)
    gram = jnp.dot(hessen.T, hessen, precision=HIGH)
    coeffs = small_solve(gram, beta * hessen[0])
    fitted = jnp.dot(hessen, coeffs, precision=HIGH)
    update = coeffs[0] * basis[0]
    for index in range(1, M):
        update = update + coeffs[index] * basis[index]
    remaining = start
    for index in range(M + 1):
        remaining = remaining - fitted[index] * basis[index]
    return (voltages + update, remaining)
```

```python
import functools
import math

import jax
import jax.numpy as jnp
import ml_dtypes
import numpy as np
from jax import lax
from jax.experimental import pallas as pl
from jax.experimental.pallas import tpu as pltpu
from jax.sharding import PartitionSpec as P

NB = 128
HALO = 3
NOFF = 7
M = 4
NTYPES = 4
G = 2
MESH = pl.DeviceIdType.MESH
F32 = jnp.float32
BF16 = jnp.bfloat16


def hartley(count):
    grid = np.arange(count)
    angle = (grid[:, None] * grid[None, :] % count) * (2.0 * math.pi / count)
    return (np.cos(angle) + np.sin(angle)) / math.sqrt(count)


def halves(matrix):
    whole = matrix.astype(np.float32)
    high = whole.astype(ml_dtypes.bfloat16)
    low = (whole - high.astype(np.float32)).astype(ml_dtypes.bfloat16)
    return np.stack([high, low])


def matrices(k1, k2, tones):
    kb, ks = k2 // tones, k1 // tones
    first = np.kron(hartley(k1), np.eye(kb))
    table = hartley(k2).reshape(k2, tones, kb)
    second = np.einsum("pq,teb->pteqb", np.eye(ks), table).reshape(ks * k2, tones * ks * kb)
    return np.stack([halves(first), halves(second), halves(second.T)])


def split(x):
    high = x.astype(BF16)
    return high, (x - high.astype(F32)).astype(BF16)


def mul(a, b):
    return jnp.dot(a, b, preferred_element_type=F32)


def kernel(
    dims,
    code_s, act_s, type_s, volt, source, coup_hbm, cap, damp, kind, mats,
    new_ref, rem_ref,
    coup, wh, wl, q, w, fsend, frecv, bsend, brecv, slope, yv, xe, halo, ar1, ar2, ar3,
    csem, fs, fr, bs, br, hs, hr, s1, r1, s2, r2, s3, r3,
):
    blocks, rows, tones, xh, zs, cores = dims
    piece = rows // tones
    chunks, half = blocks // G, min(blocks // 2, blocks - HALO)
    nodes = xh * zs * cores
    me = lax.axis_index("tone")
    node = lax.axis_index("node")
    right, left = lax.rem(node + 1, nodes), lax.rem(node + nodes - 1, nodes)
    others = [lax.rem(me + step, tones) for step in range(1, tones)]
    core, rest = lax.rem(node, cores), node // cores
    zed, far = lax.rem(rest, zs), rest // zs
    near = xh * cores
    spot = far * cores + core
    near_slots = [lax.rem(spot + step, near) for step in range(1, near)]
    near_nodes = [((slot // cores) * zs + zed) * cores + lax.rem(slot, cores) for slot in near_slots]
    z_slots = [lax.rem(zed + step, zs) for step in range(1, zs)]
    z_nodes = [(far * zs + slot) * cores + core for slot in z_slots]

    fetch = pltpu.make_async_copy(coup_hbm, coup, csem)
    fetch.start()
    barrier = pltpu.get_barrier_semaphore()
    for peer in others:
        pl.semaphore_signal(barrier, inc=1, device_id={"tone": peer}, device_id_type=MESH)
    for peer in [left, right] + near_nodes + z_nodes:
        pl.semaphore_signal(barrier, inc=1, device_id={"node": peer}, device_id_type=MESH)
    pl.semaphore_wait(barrier, len(others) + 2 + len(near_nodes) + len(z_nodes))

    def exchange(src, dst, ssem, rsem, c, to, slot):
        return pltpu.make_async_remote_copy(
            src_ref=src.at[pl.ds(c * G, G), to],
            dst_ref=dst.at[pl.ds(c * G, G), slot],
            send_sem=ssem.at[c, to],
            recv_sem=rsem.at[c, slot],
            device_id={"tone": to},
            device_id_type=MESH,
        )

    def send_chunk(src, dst, ssem, rsem, c):
        for peer in others:
            exchange(src, dst, ssem, rsem, c, peer, me).start()
        dst[pl.ds(c * G, G), pl.ds(me, 1)] = src[pl.ds(c * G, G), pl.ds(me, 1)]

    def wait_chunk(src, dst, ssem, rsem, c):
        for peer in others:
            exchange(src, dst, ssem, rsem, c, peer, peer).wait_recv()

    def wait_sent(src, dst, ssem, rsem, c):
        for peer in others:
            exchange(src, dst, ssem, rsem, c, peer, me).wait_send()

    def wide(ref, c):
        return jnp.concatenate([ref[c * G + i].reshape(rows, NB) for i in range(G)], axis=1)

    def put(ref, c, value):
        for i in range(G):
            ref[c * G + i] = value[:, i * NB : (i + 1) * NB].reshape(ref.shape[1:])

    def apply_matrix(which, high, low):
        return mul(mats[which, 0], high) + mul(mats[which, 1], high) + mul(mats[which, 0], low)

    def halo_copies(x, par):
        return [
            pltpu.make_async_remote_copy(
                src_ref=x.at[pl.ds(begin, HALO)],
                dst_ref=halo.at[par, side],
                send_sem=hs.at[par, side],
                recv_sem=hr.at[par, side],
                device_id={"node": peer},
                device_id_type=MESH,
            )
            for side, begin, peer in ((0, blocks - HALO, right), (1, 0, left))
        ]

    def take_halo(side, par, place):
        outside = (node == 0) if side == 0 else (node == nodes - 1)
        keep = jnp.where(outside, 0.0, 1.0).astype(F32)
        for i in range(HALO):
            high, low = split(halo[par, side, i] * keep)
            at = (place + i) * NB
            xe[0:rows, at : at + NB] = high
            xe[rows : 2 * rows, at : at + NB] = low

    def couple(x, begin, end):
        @pl.loop(begin, end)
        def _(r):
            lhs = xe[:, pl.ds(pl.multiple_of(r * NB, NB), NOFF * NB)]
            both = mul(lhs, wh[r])
            more = mul(lhs[0:rows], wl[r])
            yv[r] = damp[...] * cap[r] * x[r] + both[0:rows] + both[rows : 2 * rows] + more

    def spread(x):
        @pl.loop(0, chunks)
        def _(c):
            high, low = split(wide(x, c))
            at = pl.multiple_of((c * G + HALO) * NB, NB)
            xe[0:rows, pl.ds(at, G * NB)] = high
            xe[rows : 2 * rows, pl.ds(at, G * NB)] = low
            put(fsend, c, apply_matrix(0, high, low))
            send_chunk(fsend, frecv, fs, fr, c)

    def turn(middle):
        @pl.loop(0, chunks)
        def _(c):
            wait_chunk(fsend, frecv, fs, fr, c)
            field = apply_matrix(1, *split(wide(frecv, c)))
            put(bsend, c, apply_matrix(2, *split(middle(c, field))))
            send_chunk(bsend, brecv, bs, br, c)

    def landed(c):
        wait_chunk(bsend, brecv, bs, br, c)
        back = apply_matrix(0, *split(wide(brecv, c)))
        return [back[:, i * NB : (i + 1) * NB] for i in range(G)]

    def all_sent():
        @pl.loop(0, chunks)
        def _(c):
            wait_sent(fsend, frecv, fs, fr, c)
            wait_sent(bsend, brecv, bs, br, c)

    def phase(ref, par, own, slots, peers, axis, ssem, rsem, step):
        for slot, peer in zip(slots, peers):
            if step == "wait":
                there = pltpu.make_async_remote_copy(
                    src_ref=ref.at[par, own], dst_ref=ref.at[par, slot],
                    send_sem=ssem.at[par, slot], recv_sem=rsem.at[par, slot],
                    device_id={axis: peer}, device_id_type=MESH,
                )
                there.wait_recv()
                there.wait_send()
            else:
                pltpu.make_async_remote_copy(
                    src_ref=ref.at[par, own], dst_ref=ref.at[par, own],
                    send_sem=ssem.at[par, slot], recv_sem=rsem.at[par, own],
                    device_id={axis: peer}, device_id_type=MESH,
                ).start()

    one = (ar1, me, others, others, "tone", s1, r1)
    two = (ar2, spot, near_slots, near_nodes, "node", s2, r2)
    three = (ar3, zed, z_slots, z_nodes, "node", s3, r3)

    def run(stage, par, step):
        ref, own, slots, peers, axis, ssem, rsem = stage
        phase(ref, par, own, slots, peers, axis, ssem, rsem, step)

    def pass_on(before, after, par):
        run(before, par, "wait")
        ref, own = after[0], after[1]
        ref[par, own] = jnp.sum(before[0][par], axis=0)
        run(after, par, "send")

    def begin_sum(par, parts):
        lines = [jnp.sum(part, axis=0, keepdims=True) for part in parts]
        lines += [jnp.zeros((8 - len(lines), NB), F32)]
        ar1[par, me] = jnp.concatenate(lines, axis=0)
        run(one, par, "send")

    def end_sum(par, count):
        run(three, par, "wait")
        total = jnp.sum(jnp.sum(ar3[par], axis=0), axis=1, keepdims=True)
        total = jnp.broadcast_to(total, (8, NB))
        return [total[i : i + 1] for i in range(count)]

    def fold(a, b):
        return jnp.sum((a * b).reshape(rows // 8, 8, NB), axis=0)

    zero = jnp.zeros((8, NB), F32)

    def apply(x, par, middle, extra, finish, count, summing):
        for copy in halo_copies(x, par):
            copy.start()
        spread(x)
        extra()
        if summing is not None:
            pass_on(one, two, summing)
        copies = halo_copies(x, par)
        copies[0].wait_recv()
        take_halo(0, par, 0)
        couple(x, 0, half)
        turn(middle)
        if summing is not None:
            pass_on(two, three, summing)
        copies[1].wait_recv()
        take_halo(1, par, blocks + HALO)
        couple(x, half, blocks)
        scalars = finish("scalars", None)
        def body(c, parts):
            for i, value in enumerate(landed(c)):
                r = c * G + i
                news = finish(r, value + yv[r], scalars) if scalars is not None else finish(r, value + yv[r])
                parts = [a + b for a, b in zip(parts, news)]
            return parts
        parts = lax.fori_loop(0, chunks, body, [zero] * count)
        all_sent()
        for copy in copies:
            copy.wait_send()
        return parts, scalars

    def prepare():
        fetch.wait()
        bands = []
        for offset in range(NOFF):
            band = jnp.int32(0)
            for j in range(1, NOFF):
                band = jnp.where(code_s[j] == offset, j, band)
            bands.append(band)

        @pl.loop(0, blocks)
        def _(r):
            for offset in range(NOFF):
                present = act_s[r, bands[offset]].astype(F32)
                high, low = split((coup[r, bands[offset]] * present).T)
                wh[r, offset * NB : (offset + 1) * NB] = high
                wl[r, offset * NB : (offset + 1) * NB] = low

    def of_type(row, c):
        types = jnp.concatenate([kind[c * G + i] for i in range(G)], axis=1)
        value = jnp.zeros(types.shape, F32)
        for number in range(NTYPES):
            value = jnp.where(types == number, type_s[row, number], value)
        return value

    def device(c, wave):
        linear, amplitude, sharpness = (of_type(row, c) for row in range(3))
        bend = jnp.tanh(sharpness * wave)
        put(slope, c, linear + (amplitude * sharpness) * (1.0 - bend * bend))
        return linear * wave + amplitude * bend

    def tangent(c, wave):
        return wide(slope, c) * wave

    def nothing():
        pass

    def first(r, value, scalars=None):
        if r == "scalars":
            return None
        start = source[r] - value
        q[0, r] = start
        return [fold(start, start)]

    parts, _ = apply(volt, 0, device, prepare, first, 1, None)
    begin_sum(0, parts)

    columns = []
    inverse = beta = None
    for k in range(M):
        par = k % 2

        def finish(r, value, scalars=None, k=k, par=par):
            if isinstance(r, str):
                if k == 0:
                    (square,) = end_sum(par, 1)
                    root = jnp.sqrt(square)
                    return root, 1.0 / root
                return column(k - 1, par)
            if k == 0:
                new = value * scalars[1]
                w[0, r] = new
                return [fold(q[0, r], new), fold(new, new)]
            plain, scaled, inv = scalars[0], scalars[1], scalars[2]
            vector, image = w[k - 1, r], value
            for i in range(k):
                vector = vector - scaled[i] * q[i, r]
                image = image - plain[i] * w[i, r]
            vector, image = vector * inv, image * inv
            q[k, r] = vector
            w[k, r] = image
            return [fold(q[i, r], image) for i in range(k)] + [fold(vector, image), fold(image, image)]

        def column(j, par):
            sums = end_sum(par, j + 2)
            plain = [sums[0] * inverse] + sums[1 : j + 1]
            square = sums[j + 1]
            for value in plain:
                square = square - value * value
            length = jnp.sqrt(square)
            return plain, [plain[0] * inverse] + plain[1:], 1.0 / length, length

        vector = q.at[0] if k == 0 else w.at[k - 1]
        parts, scalars = apply(vector, (k + 1) % 2, tangent, nothing, finish, k + 2, par)
        if k == 0:
            beta, inverse = scalars
        else:
            columns.append(scalars)
        begin_sum((k + 1) % 2, parts)

    par = M % 2
    pass_on(one, two, par)
    pass_on(two, three, par)
    columns.append(column(M - 1, par))

    h = [[None] * M for _ in range(M + 1)]
    for j, (plain, _, _, length) in enumerate(columns):
        for i in range(j + 1):
            h[i][j] = plain[i]
        h[j + 1][j] = length

    def gram(a, b):
        terms = [h[i][a] * h[i][b] for i in range(M + 1) if h[i][a] is not None and h[i][b] is not None]
        return functools.reduce(lambda u, v: u + v, terms)

    lower = [[None] * M for _ in range(M)]
    recip = [None] * M
    for a in range(M):
        for b in range(a + 1):
            total = gram(a, b)
            for c in range(b):
                total = total - lower[a][c] * lower[b][c]
            if a == b:
                lower[a][a] = jnp.sqrt(total)
                recip[a] = 1.0 / lower[a][a]
            else:
                lower[a][b] = total * recip[b]
    forward = []
    for a in range(M):
        total = beta * h[0][a]
        for b in range(a):
            total = total - lower[a][b] * forward[b]
        forward.append(total * recip[a])
    coeffs = [None] * M
    for a in reversed(range(M)):
        total = forward[a]
        for b in range(a + 1, M):
            total = total - lower[b][a] * coeffs[b]
        coeffs[a] = total * recip[a]
    fitted = []
    for i in range(M + 1):
        terms = [h[i][j] * coeffs[j] for j in range(M) if h[i][j] is not None]
        fitted.append(functools.reduce(lambda u, v: u + v, terms))
    plain, _, inv, _ = columns[-1]
    last = fitted[M] * inv
    shares = [fitted[i] - last * plain[i] for i in range(M)]
    shares[0] = shares[0] * inverse
    steps = [coeffs[0] * inverse] + coeffs[1:]

    @pl.loop(0, blocks)
    def _(r):
        base = [q[i, r] for i in range(M)]
        value = volt[r]
        remaining = base[0] - last * w[M - 1, r]
        for i in range(M):
            value = value + steps[i] * base[i]
            remaining = remaining - shares[i] * base[i]
        new_ref[r] = value
        rem_ref[r] = remaining


def solution(mesh):
    tones, nodes = mesh.shape["tone"], mesh.shape["node"]
    cores = 2
    xh = 2 if nodes >= 32 else 1
    zs = nodes // (cores * xh)

    def per_device(voltages, source, coupling, band_code, active, cap, damp, kind, type_params):
        k1, kb, width = voltages.shape
        k2 = kb * tones
        rows, blocks, piece = k1 * kb, width // NB, k1 * kb // tones
        chunks = blocks // G

        def inward(field):
            return field.reshape(rows, blocks, NB).transpose(1, 0, 2)

        def outward(field):
            return field.transpose(1, 0, 2).reshape(k1, kb, width)

        smem = pl.BlockSpec(memory_space=pltpu.SMEM)
        vmem = pl.BlockSpec(memory_space=pltpu.VMEM)
        field = (blocks, rows, NB)
        pieces = (blocks, tones, piece, NB)
        dma = pltpu.SemaphoreType.DMA
        new, remaining = pl.pallas_call(
            functools.partial(kernel, (blocks, rows, tones, xh, zs, cores)),
            out_shape=(jax.ShapeDtypeStruct(field, F32),) * 2,
            in_specs=[smem, smem, smem, vmem, vmem, pl.BlockSpec(memory_space=pl.ANY), vmem, vmem, vmem, vmem],
            out_specs=(vmem, vmem),
            scratch_shapes=[
                pltpu.VMEM((blocks, NOFF, NB, NB), F32),
                pltpu.VMEM((blocks, NOFF * NB, NB), BF16),
                pltpu.VMEM((blocks, NOFF * NB, NB), BF16),
                pltpu.VMEM((M,) + field, F32),
                pltpu.VMEM((M,) + field, F32),
                pltpu.VMEM(pieces, F32),
                pltpu.VMEM(pieces, F32),
                pltpu.VMEM(pieces, F32),
                pltpu.VMEM(pieces, F32),
                pltpu.VMEM(field, F32),
                pltpu.VMEM(field, F32),
                pltpu.VMEM((2 * rows, (blocks + 2 * HALO) * NB), BF16),
                pltpu.VMEM((2, 2, HALO, rows, NB), F32),
                pltpu.VMEM((2, tones, 8, NB), F32),
                pltpu.VMEM((2, xh * cores, 8, NB), F32),
                pltpu.VMEM((2, zs, 8, NB), F32),
                dma,
                dma((chunks, tones)), dma((chunks, tones)),
                dma((chunks, tones)), dma((chunks, tones)),
                dma((2, 2)), dma((2, 2)),
                dma((2, tones)), dma((2, tones)),
                dma((2, xh * cores)), dma((2, xh * cores)),
                dma((2, zs)), dma((2, zs)),
            ],
            compiler_params=pltpu.CompilerParams(
                collective_id=0, has_side_effects=True, vmem_limit_bytes=56 * 1024 * 1024
            ),
        )(
            band_code, active, type_params, inward(voltages), inward(source), coupling,
            cap.reshape(blocks, 1, NB),
            jnp.broadcast_to(damp.reshape(rows, 1), (rows, NB)),
            kind.reshape(blocks, 1, NB),
            jnp.asarray(matrices(k1, k2, tones)),
        )
        return outward(new), outward(remaining)

    spread = P(None, "tone", "node")
    return jax.shard_map(
        per_device,
        mesh=mesh,
        in_specs=(
            spread, spread, P("node", None, None, None), P(), P("node", None), P("node"), P(None, "tone"), P("node"), P(),
        ),
        out_specs=(spread, spread),
        check_vma=False,
    )
```

```python
import functools
import math

import jax
import jax.numpy as jnp
import ml_dtypes
import numpy as np
from jax import lax
from jax.experimental import pallas as pl
from jax.experimental.pallas import tpu as pltpu
from jax.sharding import PartitionSpec as P

NB = 128
HALO = 3
NOFF = 7
M = 4
NTYPES = 4
G = 2
MESH = pl.DeviceIdType.MESH
F32 = jnp.float32
BF16 = jnp.bfloat16


def hartley(count):
    grid = np.arange(count)
    angle = (grid[:, None] * grid[None, :] % count) * (2.0 * math.pi / count)
    return (np.cos(angle) + np.sin(angle)) / math.sqrt(count)


def halves(matrix):
    whole = matrix.astype(np.float32)
    high = whole.astype(ml_dtypes.bfloat16)
    low = (whole - high.astype(np.float32)).astype(ml_dtypes.bfloat16)
    return np.stack([high, low])


def matrices(k1, k2, tones):
    kb, ks = k2 // tones, k1 // tones
    first = np.kron(hartley(k1), np.eye(kb))
    table = hartley(k2).reshape(k2, tones, kb)
    second = np.einsum("pq,teb->pteqb", np.eye(ks), table).reshape(ks * k2, tones * ks * kb)
    return np.stack([halves(first), halves(second), halves(second.T)])


def split(x):
    high = x.astype(BF16)
    return high, (x - high.astype(F32)).astype(BF16)


def mul(a, b):
    return jnp.dot(a, b, preferred_element_type=F32)


def kernel(
    dims,
    code_s, act_s, type_s, volt, source, coup_hbm, cap, damp, kind, mats,
    new_ref, rem_ref,
    coup, wh, wl, vold, q, w, fsend, frecv, bsend, brecv, slope, yv, xe, halo, along, across,
    csem, fs, fr, bs, br, hs, hr, s1, r1, s3, r3,
):
    blocks, rows, tones, xh, zs, cores = dims
    piece = rows // tones
    chunks = blocks // G
    nodes = xh * zs * cores
    me = lax.axis_index("tone")
    node = lax.axis_index("node")
    right, left = lax.rem(node + 1, nodes), lax.rem(node + nodes - 1, nodes)
    others = [lax.rem(me + step, tones) for step in range(1, tones)]
    core, rest = lax.rem(node, cores), node // cores
    zed, far = lax.rem(rest, zs), rest // zs
    plane = xh * cores * tones
    own = (far * cores + core) * tones + me

    def in_plane(step):
        slot = lax.rem(own + step, plane)
        spot = slot // tones
        there = ((spot // cores) * zs + zed) * cores + lax.rem(spot, cores)
        return slot, {"node": there, "tone": lax.rem(slot, tones)}

    z_slots = [lax.rem(zed + step, zs) for step in range(1, zs)]
    z_nodes = [(far * zs + slot) * cores + core for slot in z_slots]

    fetch = pltpu.make_async_copy(coup_hbm, coup, csem)
    fetch.start()
    barrier = pltpu.get_barrier_semaphore()

    @pl.loop(1, plane)
    def _(step):
        pl.semaphore_signal(barrier, inc=1, device_id=in_plane(step)[1], device_id_type=MESH)

    for peer in [left, right] + z_nodes:
        pl.semaphore_signal(barrier, inc=1, device_id={"node": peer}, device_id_type=MESH)
    partners = plane - 1 + 2 + len(z_nodes)

    def exchange(src, dst, ssem, rsem, c, to, slot):
        return pltpu.make_async_remote_copy(
            src_ref=src.at[pl.ds(c * G, G), to],
            dst_ref=dst.at[pl.ds(c * G, G), slot],
            send_sem=ssem.at[c, to],
            recv_sem=rsem.at[c, slot],
            device_id={"tone": to},
            device_id_type=MESH,
        )

    def send_chunk(src, dst, ssem, rsem, c):
        for peer in others:
            exchange(src, dst, ssem, rsem, c, peer, me).start()
        dst[pl.ds(c * G, G), pl.ds(me, 1)] = src[pl.ds(c * G, G), pl.ds(me, 1)]

    def wait_chunk(src, dst, ssem, rsem, c):
        for peer in others:
            exchange(src, dst, ssem, rsem, c, peer, peer).wait_recv()

    def wait_sent(src, dst, ssem, rsem, c):
        for peer in others:
            exchange(src, dst, ssem, rsem, c, peer, me).wait_send()

    def wide(ref, c):
        return jnp.concatenate([ref[c * G + i].reshape(rows, NB) for i in range(G)], axis=1)

    def put(ref, c, value):
        for i in range(G):
            ref[c * G + i] = value[:, i * NB : (i + 1) * NB].reshape(ref.shape[1:])

    def inner(ref, c):
        return ref[:, :, pl.ds(pl.multiple_of(c * G * NB, G * NB), G * NB)].reshape(rows, G * NB)

    def outer(ref, c, value):
        ref[:, :, pl.ds(pl.multiple_of(c * G * NB, G * NB), G * NB)] = value.reshape(ref.shape[:2] + (G * NB,))

    def over(value):
        return jnp.concatenate([value] * G, axis=1)

    def apply_matrix(which, high, low):
        return mul(mats[which, 0], high) + mul(mats[which, 1], high) + mul(mats[which, 0], low)

    def halo_copies(x, par):
        return [
            pltpu.make_async_remote_copy(
                src_ref=x.at[pl.ds(begin, HALO)],
                dst_ref=halo.at[par, side],
                send_sem=hs.at[par, side],
                recv_sem=hr.at[par, side],
                device_id={"node": peer},
                device_id_type=MESH,
            )
            for side, begin, peer in ((0, blocks - HALO, right), (1, 0, left))
        ]

    def take_halo(side, par, place):
        outside = (node == 0) if side == 0 else (node == nodes - 1)
        keep = jnp.where(outside, 0.0, 1.0).astype(F32)
        for i in range(HALO):
            high, low = split(halo[par, side, i] * keep)
            at = (place + i) * NB
            xe[0:rows, at : at + NB] = high
            xe[rows : 2 * rows, at : at + NB] = low

    def couple(x, begin, end):
        @pl.loop(begin, end)
        def _(r):
            lhs = xe[:, pl.ds(pl.multiple_of(r * NB, NB), NOFF * NB)]
            both = mul(lhs, wh[r])
            more = mul(lhs[0:rows], wl[r])
            yv[r] = damp[...] * cap[r] * x[r] + both[0:rows] + both[rows : 2 * rows] + more

    def transform(c, value):
        high, low = split(value)
        at = pl.multiple_of((c * G + HALO) * NB, NB)
        xe[0:rows, pl.ds(at, G * NB)] = high
        xe[rows : 2 * rows, pl.ds(at, G * NB)] = low
        put(fsend, c, apply_matrix(0, high, low))

    def turn(middle, begin, end):
        @pl.loop(begin, end)
        def _(c):
            wait_chunk(fsend, frecv, fs, fr, c)
            field = apply_matrix(1, *split(wide(frecv, c)))
            put(bsend, c, apply_matrix(2, *split(middle(c, field))))
            send_chunk(bsend, brecv, bs, br, c)

    lane = lax.broadcasted_iota(jnp.int32, (1, NB), 1)

    def small(ref, par, mine, slot, landing, ssem, rsem, where):
        return pltpu.make_async_remote_copy(
            src_ref=ref.at[par, mine], dst_ref=ref.at[par, landing],
            send_sem=ssem.at[par, slot], recv_sem=rsem.at[par, landing],
            device_id=where, device_id_type=MESH,
        )

    def begin_sum(par, parts):
        row = jnp.zeros((1, NB), F32)
        for i, part in enumerate(parts):
            line = jnp.sum(part, axis=0, keepdims=True)
            row = jnp.where(lane == i, jnp.sum(line, axis=1, keepdims=True), row)
        along[par, zed] = row
        for slot, peer in zip(z_slots, z_nodes):
            small(along, par, zed, slot, zed, s3, r3, {"node": peer}).start()

    def pass_on(par):
        for slot, peer in zip(z_slots, z_nodes):
            there = small(along, par, zed, slot, slot, s3, r3, {"node": peer})
            there.wait_recv()
            there.wait_send()
        across[par, own] = jnp.sum(along[par], axis=0)

        @pl.loop(1, plane)
        def _(step):
            slot, where = in_plane(step)
            small(across, par, own, slot, own, s1, r1, where).start()

    def end_sum(par, count):
        @pl.loop(1, plane)
        def _(step):
            slot, where = in_plane(step)
            there = small(across, par, own, slot, slot, s1, r1, where)
            there.wait_recv()
            there.wait_send()

        total = jnp.sum(across[par], axis=0)
        picked = [jnp.sum(jnp.where(lane == i, total, 0.0), axis=1, keepdims=True) for i in range(count)]
        return [jnp.broadcast_to(value, (1, NB)) for value in picked]

    def fold(a, b):
        return jnp.sum((a * b).reshape(rows // 8, 8, G * NB), axis=0)

    zero = jnp.zeros((8, G * NB), F32)

    def advance(step, target, count, onward=True):
        def body(c, parts):
            wait_chunk(bsend, brecv, bs, br, c)
            back = apply_matrix(0, *split(wide(brecv, c)))
            new, news = step(c, wide(yv, c) + back)
            put(target, c, new)
            wait_sent(fsend, frecv, fs, fr, c)
            wait_sent(bsend, brecv, bs, br, c)
            if onward:
                transform(c, new)
                send_chunk(fsend, frecv, fs, fr, c)
            return [a + b for a, b in zip(parts, news)]

        return lax.fori_loop(0, chunks, body, [zero] * count)

    def apply(x, par, middle, late, summing):
        up, down = halo_copies(x, par)
        up.start()
        down.start()
        couple(x, HALO, blocks - HALO)
        turn(middle, 0, 1)
        if summing is not None:
            pass_on(summing)
        turn(middle, 1, chunks)
        late()
        up.wait_recv()
        take_halo(0, par, 0)
        couple(x, 0, HALO)
        down.wait_recv()
        take_halo(1, par, blocks + HALO)
        couple(x, blocks - HALO, blocks)
        up.wait_send()
        down.wait_send()

    def prepare(begin, end):
        bands = []
        for offset in range(NOFF):
            band = jnp.int32(0)
            for j in range(1, NOFF):
                band = jnp.where(code_s[j] == offset, j, band)
            bands.append(band)

        @pl.loop(begin, end)
        def _(r):
            for offset in range(NOFF):
                present = act_s[r, bands[offset]].astype(F32)
                high, low = split((coup[r, bands[offset]] * present).T)
                wh[r, offset * NB : (offset + 1) * NB] = high
                wl[r, offset * NB : (offset + 1) * NB] = low

    def of_type(row, c):
        types = jnp.concatenate([kind[c * G + i] for i in range(G)], axis=1)
        value = jnp.zeros(types.shape, F32)
        for number in range(NTYPES):
            value = jnp.where(types == number, type_s[row, number], value)
        return value

    def device(c, wave):
        linear, amplitude, sharpness = (of_type(row, c) for row in range(3))
        bend = jnp.tanh(sharpness * wave)
        put(slope, c, linear + (amplitude * sharpness) * (1.0 - bend * bend))
        return linear * wave + amplitude * bend

    def tangent(c, wave):
        return wide(slope, c) * wave

    def nothing():
        pass

    @pl.loop(0, chunks)
    def _(c):
        value = inner(volt, c)
        put(vold, c, value)
        transform(c, value)

    fetch.wait()
    prepare(0, blocks - HALO)
    pl.semaphore_wait(barrier, partners)

    @pl.loop(0, chunks)
    def _(c):
        send_chunk(fsend, frecv, fs, fr, c)

    @pl.loop(0, chunks)
    def _(c):
        put(q.at[0], c, inner(source, c))

    apply(vold, 0, device, lambda: prepare(blocks - HALO, blocks), None)

    def residual(c, value):
        start = wide(q.at[0], c) - value
        return start, [fold(start, start)]

    begin_sum(0, advance(residual, q.at[0], 1))

    def column(j, par):
        sums = end_sum(par, j + 2)
        plain = [sums[0] * inverse] + sums[1 : j + 1]
        square = sums[j + 1]
        for value in plain:
            square = square - value * value
        length = jnp.sqrt(square)
        return plain, [plain[0] * inverse] + plain[1:], 1.0 / length, length

    apply(q.at[0], 1, tangent, nothing, 0)
    (square,) = end_sum(0, 1)
    beta = jnp.sqrt(square)
    inverse = 1.0 / beta

    def initial(c, value):
        image = value * over(inverse)
        return image, [fold(wide(q.at[0], c), image), fold(image, image)]

    begin_sum(1, advance(initial, w.at[0], 2))

    columns = []
    for k in range(1, M):
        apply(w.at[k - 1], (k + 1) % 2, tangent, nothing, k % 2)
        columns.append(column(k - 1, k % 2))
        plain, scaled, inv, _ = columns[-1]

        def following(c, image, k=k, plain=plain, scaled=scaled, inv=inv):
            vector = wide(w.at[k - 1], c)
            base = [wide(q.at[i], c) for i in range(k)]
            for i in range(k):
                vector = vector - over(scaled[i]) * base[i]
                image = image - over(plain[i]) * wide(w.at[i], c)
            vector, image = vector * over(inv), image * over(inv)
            put(q.at[k], c, vector)
            return image, [fold(b, image) for b in base + [vector, image]]

        begin_sum((k + 1) % 2, advance(following, w.at[k], k + 2, k < M - 1))

    par = M % 2
    pass_on(par)
    columns.append(column(M - 1, par))

    h = [[None] * M for _ in range(M + 1)]
    for j, (plain, _, _, length) in enumerate(columns):
        for i in range(j + 1):
            h[i][j] = plain[i]
        h[j + 1][j] = length

    def gram(a, b):
        terms = [h[i][a] * h[i][b] for i in range(M + 1) if h[i][a] is not None and h[i][b] is not None]
        return functools.reduce(lambda u, v: u + v, terms)

    lower = [[None] * M for _ in range(M)]
    recip = [None] * M
    for a in range(M):
        for b in range(a + 1):
            total = gram(a, b)
            for c in range(b):
                total = total - lower[a][c] * lower[b][c]
            if a == b:
                lower[a][a] = jnp.sqrt(total)
                recip[a] = 1.0 / lower[a][a]
            else:
                lower[a][b] = total * recip[b]
    forward = []
    for a in range(M):
        total = beta * h[0][a]
        for b in range(a):
            total = total - lower[a][b] * forward[b]
        forward.append(total * recip[a])
    coeffs = [None] * M
    for a in reversed(range(M)):
        total = forward[a]
        for b in range(a + 1, M):
            total = total - lower[b][a] * coeffs[b]
        coeffs[a] = total * recip[a]
    fitted = []
    for i in range(M + 1):
        terms = [h[i][j] * coeffs[j] for j in range(M) if h[i][j] is not None]
        fitted.append(functools.reduce(lambda u, v: u + v, terms))
    plain, _, inv, _ = columns[-1]
    last = fitted[M] * inv
    shares = [fitted[i] - last * plain[i] for i in range(M)]
    shares[0] = shares[0] * inverse
    steps = [coeffs[0] * inverse] + coeffs[1:]

    @pl.loop(0, chunks)
    def _(c):
        base = [wide(q.at[i], c) for i in range(M)]
        value = wide(vold, c)
        remaining = base[0] - over(last) * wide(w.at[M - 1], c)
        for i in range(M):
            value = value + over(steps[i]) * base[i]
            remaining = remaining - over(shares[i]) * base[i]
        outer(new_ref, c, value)
        outer(rem_ref, c, remaining)


def solution(mesh):
    tones, nodes = mesh.shape["tone"], mesh.shape["node"]
    cores = 2
    xh = 2 if nodes >= 32 else 1
    zs = nodes // (cores * xh)

    def per_device(voltages, source, coupling, band_code, active, cap, damp, kind, type_params):
        k1, kb, width = voltages.shape
        k2 = kb * tones
        rows, blocks, piece = k1 * kb, width // NB, k1 * kb // tones
        chunks = blocks // G

        smem = pl.BlockSpec(memory_space=pltpu.SMEM)
        vmem = pl.BlockSpec(memory_space=pltpu.VMEM)
        field = (blocks, rows, NB)
        pieces = (blocks, tones, piece, NB)
        dma = pltpu.SemaphoreType.DMA
        new, remaining = pl.pallas_call(
            functools.partial(kernel, (blocks, rows, tones, xh, zs, cores)),
            out_shape=(jax.ShapeDtypeStruct(voltages.shape, F32),) * 2,
            in_specs=[smem, smem, smem, vmem, vmem, pl.BlockSpec(memory_space=pl.ANY), vmem, vmem, vmem, vmem],
            out_specs=(vmem, vmem),
            scratch_shapes=[
                pltpu.VMEM((blocks, NOFF, NB, NB), F32),
                pltpu.VMEM((blocks, NOFF * NB, NB), BF16),
                pltpu.VMEM((blocks, NOFF * NB, NB), BF16),
                pltpu.VMEM(field, F32),
                pltpu.VMEM((M,) + field, F32),
                pltpu.VMEM((M,) + field, F32),
                pltpu.VMEM(pieces, F32),
                pltpu.VMEM(pieces, F32),
                pltpu.VMEM(pieces, F32),
                pltpu.VMEM(pieces, F32),
                pltpu.VMEM(field, F32),
                pltpu.VMEM(field, F32),
                pltpu.VMEM((2 * rows, (blocks + 2 * HALO) * NB), BF16),
                pltpu.VMEM((2, 2, HALO, rows, NB), F32),
                pltpu.VMEM((2, zs, 1, NB), F32),
                pltpu.VMEM((2, xh * cores * tones, 1, NB), F32),
                dma,
                dma((chunks, tones)), dma((chunks, tones)),
                dma((chunks, tones)), dma((chunks, tones)),
                dma((2, 2)), dma((2, 2)),
                dma((2, xh * cores * tones)), dma((2, xh * cores * tones)),
                dma((2, zs)), dma((2, zs)),
            ],
            compiler_params=pltpu.CompilerParams(
                collective_id=0, has_side_effects=True, vmem_limit_bytes=56 * 1024 * 1024
            ),
        )(
            band_code, active, type_params, voltages, source, coupling,
            cap.reshape(blocks, 1, NB),
            jnp.broadcast_to(damp.reshape(rows, 1), (rows, NB)),
            kind.reshape(blocks, 1, NB),
            jnp.asarray(matrices(k1, k2, tones)),
        )
        return new, remaining

    spread = P(None, "tone", "node")
    return jax.shard_map(
        per_device,
        mesh=mesh,
        in_specs=(
            spread, spread, P("node", None, None, None), P(), P("node", None), P("node"), P(None, "tone"), P("node"), P(),
        ),
        out_specs=(spread, spread),
        check_vma=False,
    )
```

```python
import functools
import math

import jax
import jax.numpy as jnp
import ml_dtypes
import numpy as np
from jax import lax
from jax.experimental import pallas as pl
from jax.experimental.pallas import tpu as pltpu
from jax.sharding import PartitionSpec as P

NB = 128
HALO = 3
NOFF = 7
M = 4
NTYPES = 4
G = 2
MESH = pl.DeviceIdType.MESH
F32 = jnp.float32
BF16 = jnp.bfloat16


def hartley(count):
    grid = np.arange(count)
    angle = (grid[:, None] * grid[None, :] % count) * (2.0 * math.pi / count)
    return (np.cos(angle) + np.sin(angle)) / math.sqrt(count)


def halves(matrix):
    whole = matrix.astype(np.float32)
    high = whole.astype(ml_dtypes.bfloat16)
    low = (whole - high.astype(np.float32)).astype(ml_dtypes.bfloat16)
    return np.stack([high, low])


def matrices(k1, k2, tones):
    kb, ks = k2 // tones, k1 // tones
    first = np.kron(hartley(k1), np.eye(kb))
    table = hartley(k2).reshape(k2, tones, kb)
    second = np.einsum("pq,teb->pteqb", np.eye(ks), table).reshape(ks * k2, tones * ks * kb)
    return np.stack([halves(first), halves(second), halves(second.T)])


def split(x):
    high = x.astype(BF16)
    return high, (x - high.astype(F32)).astype(BF16)


def mul(a, b):
    return jnp.dot(a, b, preferred_element_type=F32)


def kernel(
    dims,
    code_s, act_s, type_s, volt, source, coup_hbm, cap, damp, kind, mats,
    new_ref, rem_ref,
    coup, wh, wl, vold, q, w, fsend, frecv, bsend, brecv, slope, yv, xe, halo, along, across,
    csem, fs, fr, bs, br, hs, hr, s1, r1, s3, r3,
):
    blocks, rows, tones, xh, zs, cores = dims
    piece = rows // tones
    chunks = blocks // G
    nodes = xh * zs * cores
    me = lax.axis_index("tone")
    node = lax.axis_index("node")
    right, left = lax.rem(node + 1, nodes), lax.rem(node + nodes - 1, nodes)
    ys = tones // 2
    column, place = me // ys, lax.rem(me, ys)
    hops = sorted(range(ys), key=lambda step: -min(step, ys - step))
    others = [
        (column if same else 1 - column) * ys + lax.rem(place + step, ys)
        for same in (False, True) for step in hops if not (same and step == 0)
    ]
    core, rest = lax.rem(node, cores), node // cores
    zed, far = lax.rem(rest, zs), rest // zs
    plane = xh * cores * tones
    own = (far * cores + core) * tones + me

    def in_plane(step):
        slot = lax.rem(own + step, plane)
        spot = slot // tones
        there = ((spot // cores) * zs + zed) * cores + lax.rem(spot, cores)
        return slot, {"node": there, "tone": lax.rem(slot, tones)}

    z_slots = [lax.rem(zed + step, zs) for step in range(1, zs)]
    z_nodes = [(far * zs + slot) * cores + core for slot in z_slots]

    fetch = pltpu.make_async_copy(coup_hbm, coup, csem)
    fetch.start()
    barrier = pltpu.get_barrier_semaphore()

    @pl.loop(1, plane)
    def _(step):
        pl.semaphore_signal(barrier, inc=1, device_id=in_plane(step)[1], device_id_type=MESH)

    for peer in [left, right] + z_nodes:
        pl.semaphore_signal(barrier, inc=1, device_id={"node": peer}, device_id_type=MESH)
    partners = plane - 1 + 2 + len(z_nodes)

    def exchange(src, dst, ssem, rsem, c, to, slot):
        return pltpu.make_async_remote_copy(
            src_ref=src.at[pl.ds(c * G, G), to],
            dst_ref=dst.at[pl.ds(c * G, G), slot],
            send_sem=ssem.at[c, to],
            recv_sem=rsem.at[c, slot],
            device_id={"tone": to},
            device_id_type=MESH,
        )

    def send_chunk(src, dst, ssem, rsem, c):
        for peer in others:
            exchange(src, dst, ssem, rsem, c, peer, me).start()
        dst[pl.ds(c * G, G), pl.ds(me, 1)] = src[pl.ds(c * G, G), pl.ds(me, 1)]

    def wait_chunk(src, dst, ssem, rsem, c):
        for peer in others:
            exchange(src, dst, ssem, rsem, c, peer, peer).wait_recv()

    def wait_sent(src, dst, ssem, rsem, c):
        for peer in others:
            exchange(src, dst, ssem, rsem, c, peer, me).wait_send()

    def wide(ref, c):
        return jnp.concatenate([ref[c * G + i].reshape(rows, NB) for i in range(G)], axis=1)

    def put(ref, c, value):
        for i in range(G):
            ref[c * G + i] = value[:, i * NB : (i + 1) * NB].reshape(ref.shape[1:])

    def inner(ref, c):
        return ref[:, :, pl.ds(pl.multiple_of(c * G * NB, G * NB), G * NB)].reshape(rows, G * NB)

    def outer(ref, c, value):
        ref[:, :, pl.ds(pl.multiple_of(c * G * NB, G * NB), G * NB)] = value.reshape(ref.shape[:2] + (G * NB,))

    def over(value):
        return jnp.concatenate([value] * G, axis=1)

    def apply_matrix(which, high, low):
        return mul(mats[which, 0], high) + mul(mats[which, 1], high) + mul(mats[which, 0], low)

    def halo_copies(x, par):
        return [
            pltpu.make_async_remote_copy(
                src_ref=x.at[pl.ds(begin, HALO)],
                dst_ref=halo.at[par, side],
                send_sem=hs.at[par, side],
                recv_sem=hr.at[par, side],
                device_id={"node": peer},
                device_id_type=MESH,
            )
            for side, begin, peer in ((0, blocks - HALO, right), (1, 0, left))
        ]

    def take_halo(side, par, place):
        outside = (node == 0) if side == 0 else (node == nodes - 1)
        keep = jnp.where(outside, 0.0, 1.0).astype(F32)
        for i in range(HALO):
            high, low = split(halo[par, side, i] * keep)
            at = (place + i) * NB
            xe[0:rows, at : at + NB] = high
            xe[rows : 2 * rows, at : at + NB] = low

    def couple(x, begin, end):
        @pl.loop(begin, end)
        def _(r):
            lhs = xe[:, pl.ds(pl.multiple_of(r * NB, NB), NOFF * NB)]
            both = mul(lhs, wh[r])
            more = mul(lhs[0:rows], wl[r])
            yv[r] = damp[...] * cap[r] * x[r] + both[0:rows] + both[rows : 2 * rows] + more

    def transform(c, value):
        high, low = split(value)
        at = pl.multiple_of((c * G + HALO) * NB, NB)
        xe[0:rows, pl.ds(at, G * NB)] = high
        xe[rows : 2 * rows, pl.ds(at, G * NB)] = low
        put(fsend, c, apply_matrix(0, high, low))

    def turn(middle, begin, end):
        @pl.loop(begin, end)
        def _(c):
            wait_chunk(fsend, frecv, fs, fr, c)
            field = apply_matrix(1, *split(wide(frecv, c)))
            put(bsend, c, apply_matrix(2, *split(middle(c, field))))
            send_chunk(bsend, brecv, bs, br, c)

    lane = lax.broadcasted_iota(jnp.int32, (1, NB), 1)

    def small(ref, par, mine, slot, landing, ssem, rsem, where):
        return pltpu.make_async_remote_copy(
            src_ref=ref.at[par, mine], dst_ref=ref.at[par, landing],
            send_sem=ssem.at[par, slot], recv_sem=rsem.at[par, landing],
            device_id=where, device_id_type=MESH,
        )

    def begin_sum(par, parts):
        row = jnp.zeros((1, NB), F32)
        for i, part in enumerate(parts):
            line = jnp.sum(part, axis=0, keepdims=True)
            row = jnp.where(lane == i, jnp.sum(line, axis=1, keepdims=True), row)
        along[par, zed] = row
        for slot, peer in zip(z_slots, z_nodes):
            small(along, par, zed, slot, zed, s3, r3, {"node": peer}).start()

    def pass_on(par):
        for slot, peer in zip(z_slots, z_nodes):
            there = small(along, par, zed, slot, slot, s3, r3, {"node": peer})
            there.wait_recv()
            there.wait_send()
        across[par, own] = jnp.sum(along[par], axis=0)

        @pl.loop(1, plane)
        def _(step):
            slot, where = in_plane(step)
            small(across, par, own, slot, own, s1, r1, where).start()

    def end_sum(par, count):
        @pl.loop(1, plane)
        def _(step):
            slot, where = in_plane(step)
            there = small(across, par, own, slot, slot, s1, r1, where)
            there.wait_recv()
            there.wait_send()

        total = jnp.sum(across[par], axis=0)
        picked = [jnp.sum(jnp.where(lane == i, total, 0.0), axis=1, keepdims=True) for i in range(count)]
        return [jnp.broadcast_to(value, (1, NB)) for value in picked]

    def fold(a, b):
        return jnp.sum((a * b).reshape(rows // 8, 8, G * NB), axis=0)

    zero = jnp.zeros((8, G * NB), F32)

    def advance(step, target, count, onward=True):
        def body(c, parts):
            wait_chunk(bsend, brecv, bs, br, c)
            back = apply_matrix(0, *split(wide(brecv, c)))
            new, news = step(c, wide(yv, c) + back)
            put(target, c, new)
            wait_sent(fsend, frecv, fs, fr, c)
            wait_sent(bsend, brecv, bs, br, c)
            if onward:
                transform(c, new)
                send_chunk(fsend, frecv, fs, fr, c)
            return [a + b for a, b in zip(parts, news)]

        return lax.fori_loop(0, chunks, body, [zero] * count)

    def apply(x, par, middle, late, summing):
        up, down = halo_copies(x, par)
        up.start()
        down.start()
        couple(x, HALO, blocks - HALO)
        turn(middle, 0, 1)
        if summing is not None:
            pass_on(summing)
        turn(middle, 1, chunks)
        late()
        up.wait_recv()
        take_halo(0, par, 0)
        couple(x, 0, HALO)
        down.wait_recv()
        take_halo(1, par, blocks + HALO)
        couple(x, blocks - HALO, blocks)
        up.wait_send()
        down.wait_send()

    def prepare(begin, end):
        bands = []
        for offset in range(NOFF):
            band = jnp.int32(0)
            for j in range(1, NOFF):
                band = jnp.where(code_s[j] == offset, j, band)
            bands.append(band)

        @pl.loop(begin, end)
        def _(r):
            for offset in range(NOFF):
                present = act_s[r, bands[offset]].astype(F32)
                high, low = split((coup[r, bands[offset]] * present).T)
                wh[r, offset * NB : (offset + 1) * NB] = high
                wl[r, offset * NB : (offset + 1) * NB] = low

    def of_type(row, c):
        types = jnp.concatenate([kind[c * G + i] for i in range(G)], axis=1)
        value = jnp.zeros(types.shape, F32)
        for number in range(NTYPES):
            value = jnp.where(types == number, type_s[row, number], value)
        return value

    def device(c, wave):
        linear, amplitude, sharpness = (of_type(row, c) for row in range(3))
        bend = jnp.tanh(sharpness * wave)
        put(slope, c, linear + (amplitude * sharpness) * (1.0 - bend * bend))
        return linear * wave + amplitude * bend

    def tangent(c, wave):
        return wide(slope, c) * wave

    def nothing():
        pass

    @pl.loop(0, chunks)
    def _(c):
        value = inner(volt, c)
        put(vold, c, value)
        transform(c, value)

    fetch.wait()
    prepare(0, blocks - HALO)
    pl.semaphore_wait(barrier, partners)

    @pl.loop(0, chunks)
    def _(c):
        send_chunk(fsend, frecv, fs, fr, c)

    @pl.loop(0, chunks)
    def _(c):
        put(q.at[0], c, inner(source, c))

    apply(vold, 0, device, lambda: prepare(blocks - HALO, blocks), None)

    def residual(c, value):
        start = wide(q.at[0], c) - value
        return start, [fold(start, start)]

    begin_sum(0, advance(residual, q.at[0], 1))

    def column(j, par):
        sums = end_sum(par, j + 2)
        plain = [sums[0] * inverse] + sums[1 : j + 1]
        square = sums[j + 1]
        for value in plain:
            square = square - value * value
        length = jnp.sqrt(square)
        return plain, [plain[0] * inverse] + plain[1:], 1.0 / length, length

    apply(q.at[0], 1, tangent, nothing, 0)
    (square,) = end_sum(0, 1)
    beta = jnp.sqrt(square)
    inverse = 1.0 / beta

    def initial(c, value):
        image = value * over(inverse)
        return image, [fold(wide(q.at[0], c), image), fold(image, image)]

    begin_sum(1, advance(initial, w.at[0], 2))

    columns = []
    for k in range(1, M):
        apply(w.at[k - 1], (k + 1) % 2, tangent, nothing, k % 2)
        columns.append(column(k - 1, k % 2))
        plain, scaled, inv, _ = columns[-1]

        def following(c, image, k=k, plain=plain, scaled=scaled, inv=inv):
            vector = wide(w.at[k - 1], c)
            base = [wide(q.at[i], c) for i in range(k)]
            for i in range(k):
                vector = vector - over(scaled[i]) * base[i]
                image = image - over(plain[i]) * wide(w.at[i], c)
            vector, image = vector * over(inv), image * over(inv)
            put(q.at[k], c, vector)
            return image, [fold(b, image) for b in base + [vector, image]]

        begin_sum((k + 1) % 2, advance(following, w.at[k], k + 2, k < M - 1))

    par = M % 2
    pass_on(par)
    columns.append(column(M - 1, par))

    h = [[None] * M for _ in range(M + 1)]
    for j, (plain, _, _, length) in enumerate(columns):
        for i in range(j + 1):
            h[i][j] = plain[i]
        h[j + 1][j] = length

    def gram(a, b):
        terms = [h[i][a] * h[i][b] for i in range(M + 1) if h[i][a] is not None and h[i][b] is not None]
        return functools.reduce(lambda u, v: u + v, terms)

    lower = [[None] * M for _ in range(M)]
    recip = [None] * M
    for a in range(M):
        for b in range(a + 1):
            total = gram(a, b)
            for c in range(b):
                total = total - lower[a][c] * lower[b][c]
            if a == b:
                lower[a][a] = jnp.sqrt(total)
                recip[a] = 1.0 / lower[a][a]
            else:
                lower[a][b] = total * recip[b]
    forward = []
    for a in range(M):
        total = beta * h[0][a]
        for b in range(a):
            total = total - lower[a][b] * forward[b]
        forward.append(total * recip[a])
    coeffs = [None] * M
    for a in reversed(range(M)):
        total = forward[a]
        for b in range(a + 1, M):
            total = total - lower[b][a] * coeffs[b]
        coeffs[a] = total * recip[a]
    fitted = []
    for i in range(M + 1):
        terms = [h[i][j] * coeffs[j] for j in range(M) if h[i][j] is not None]
        fitted.append(functools.reduce(lambda u, v: u + v, terms))
    plain, _, inv, _ = columns[-1]
    last = fitted[M] * inv
    shares = [fitted[i] - last * plain[i] for i in range(M)]
    shares[0] = shares[0] * inverse
    steps = [coeffs[0] * inverse] + coeffs[1:]

    @pl.loop(0, chunks)
    def _(c):
        base = [wide(q.at[i], c) for i in range(M)]
        value = wide(vold, c)
        remaining = base[0] - over(last) * wide(w.at[M - 1], c)
        for i in range(M):
            value = value + over(steps[i]) * base[i]
            remaining = remaining - over(shares[i]) * base[i]
        outer(new_ref, c, value)
        outer(rem_ref, c, remaining)


def solution(mesh):
    tones, nodes = mesh.shape["tone"], mesh.shape["node"]
    cores = 2
    xh = 2 if nodes >= 32 else 1
    zs = nodes // (cores * xh)

    def per_device(voltages, source, coupling, band_code, active, cap, damp, kind, type_params):
        k1, kb, width = voltages.shape
        k2 = kb * tones
        rows, blocks, piece = k1 * kb, width // NB, k1 * kb // tones
        chunks = blocks // G

        smem = pl.BlockSpec(memory_space=pltpu.SMEM)
        vmem = pl.BlockSpec(memory_space=pltpu.VMEM)
        field = (blocks, rows, NB)
        pieces = (blocks, tones, piece, NB)
        dma = pltpu.SemaphoreType.DMA
        new, remaining = pl.pallas_call(
            functools.partial(kernel, (blocks, rows, tones, xh, zs, cores)),
            out_shape=(jax.ShapeDtypeStruct(voltages.shape, F32),) * 2,
            in_specs=[smem, smem, smem, vmem, vmem, pl.BlockSpec(memory_space=pl.ANY), vmem, vmem, vmem, vmem],
            out_specs=(vmem, vmem),
            scratch_shapes=[
                pltpu.VMEM((blocks, NOFF, NB, NB), F32),
                pltpu.VMEM((blocks, NOFF * NB, NB), BF16),
                pltpu.VMEM((blocks, NOFF * NB, NB), BF16),
                pltpu.VMEM(field, F32),
                pltpu.VMEM((M,) + field, F32),
                pltpu.VMEM((M,) + field, F32),
                pltpu.VMEM(pieces, F32),
                pltpu.VMEM(pieces, F32),
                pltpu.VMEM(pieces, F32),
                pltpu.VMEM(pieces, F32),
                pltpu.VMEM(field, F32),
                pltpu.VMEM(field, F32),
                pltpu.VMEM((2 * rows, (blocks + 2 * HALO) * NB), BF16),
                pltpu.VMEM((2, 2, HALO, rows, NB), F32),
                pltpu.VMEM((2, zs, 1, NB), F32),
                pltpu.VMEM((2, xh * cores * tones, 1, NB), F32),
                dma,
                dma((chunks, tones)), dma((chunks, tones)),
                dma((chunks, tones)), dma((chunks, tones)),
                dma((2, 2)), dma((2, 2)),
                dma((2, xh * cores * tones)), dma((2, xh * cores * tones)),
                dma((2, zs)), dma((2, zs)),
            ],
            compiler_params=pltpu.CompilerParams(
                collective_id=0, has_side_effects=True, vmem_limit_bytes=56 * 1024 * 1024
            ),
        )(
            band_code, active, type_params, voltages, source, coupling,
            cap.reshape(blocks, 1, NB),
            jnp.broadcast_to(damp.reshape(rows, 1), (rows, NB)),
            kind.reshape(blocks, 1, NB),
            jnp.asarray(matrices(k1, k2, tones)),
        )
        return new, remaining

    spread = P(None, "tone", "node")
    return jax.shard_map(
        per_device,
        mesh=mesh,
        in_specs=(
            spread, spread, P("node", None, None, None), P(), P("node", None), P("node"), P(None, "tone"), P("node"), P(),
        ),
        out_specs=(spread, spread),
        check_vma=False,
    )
```
